32 devices in a mesh: run: 4 (over x, core), space: 8 (over z, y).
Axes of the slice: x: 2, y: 2, z: 4, core: 2. Of those that a mesh axis runs over, the one named last changes fastest.
Arguments:
- adjoint_init: float32 [4, 3, 32, 192, 256], P('run', None, 'space'), may hold values from -6 to 6
- forward_snaps: bfloat16 [8, 3, 32, 192, 256], P('run', None, 'space'), may hold values from -6 to 6
- base_speed: float32 [192], replicated, may hold values from 0.2 to 1.5
- fwd_times: int32 [8], replicated, may hold values from 0 to 15
- adj_times: int32 [4, 4], P('run'), may hold values from 0 to 15
- horizon: int32 [4], P('run'), may hold values from 8 to 24
Outputs:
- final_adjoint: float32 [4, 3, 32, 192, 256], P('run', None, 'space')
- hankel: float32 [4, 4, 8], P('run')
The draws below stay inside these ranges and needn't reach their ends.
All inputs are finite; a program needn't handle non-finite values.
Results may differ from the reference program's by a relative error of at most 0.0027.
Values may be sent and summed in bfloat16 or wider, within the bound.
No kernel may reach another device: no remote copies, remote signals or barrier semaphores. Data moves between devices by JAX's collectives and lax.ppermute only.
A program may use at most 128 MiB of HBM per device.

```python
import math
import jax
import jax.numpy as jnp
from jax import lax

NY = 192
NZ = 256
SNAP = 4
NFWD = 8
RUNS = 4
NX = 32


def touch_ends(values, own_key, low, top_value):
    longest = values.shape.index(max(values.shape))
    spots = []
    for shift in (0, 1):
        where = [jax.random.randint(jax.random.fold_in(own_key, axis), (), 0, length) for axis, length in enumerate(values.shape)]
        where[longest] = (where[longest] + shift) % values.shape[longest]
        spots.append(tuple(where))
    return values.at[spots[0]].set(low).at[spots[1]].set(top_value)


def block_levels(key, extent, cuts, low, largest):
    gain, own = 1.0, jax.random.fold_in(key, 6)
    for position, parts in cuts:
        heights = jnp.exp(jax.random.uniform(jax.random.fold_in(own, position), (parts,), jnp.float32, low / len(cuts), largest / len(cuts)))
        gain = gain * jnp.repeat(heights, extent[position] // parts).reshape([-1 if axis == position else 1 for axis in range(len(extent))])
    return gain


def bell_draw(stream_key, dims, width, limit, shards=(), dtype=jnp.bfloat16):
    values = jax.random.normal(stream_key, dims, jnp.float32) * width
    if len(shards) > 0:
        values = block_levels(stream_key, dims, shards, -0.22, 0.18) * values
    return jnp.clip(values, min=-limit, max=limit).astype(dtype)


def setup_inputs(seed: int = 0) -> dict:
    key_of = jax.random.split(jax.random.key(seed), 7)
    return {
        "adjoint_init": bell_draw(key_of[0], (RUNS, 3, NX, NY, NZ), 1.0, 6.0, ((0, 4), (2, 8)), jnp.float32),
        "forward_snaps": bell_draw(key_of[1], (NFWD, 3, NX, NY, NZ), 1.0, 6.0, ((0, 4), (2, 8))),
        "base_speed": jnp.clip(jax.random.uniform(key_of[2], (NY,), jnp.float32, 0.2, 1.5), 0.2, 1.5),
        "fwd_times": touch_ends(jax.random.randint(key_of[3], (NFWD,), 0, 16), jax.random.fold_in(key_of[3], 1), 0, 15).astype(jnp.int32),
        "adj_times": touch_ends(jax.random.randint(key_of[4], (RUNS, SNAP), 0, 16), jax.random.fold_in(key_of[4], 1), 0, 15).astype(jnp.int32),
        "horizon": touch_ends(jax.random.randint(key_of[5], (RUNS,), 8, 25), jax.random.fold_in(key_of[5], 1), 8, 24).astype(jnp.int32),
    }


time_step = 0.5
viscosity = 0.2

def operate_rim(extended, velocity, shear_rate):
    centre = extended[..., 1:-1, :, :]
    east_side = extended[..., 2:, :, :]
    west_side = extended[..., :-2, :, :]
    padded = jnp.pad(centre, [(0, 0)] * (centre.ndim - 2) + [(1, 1), (0, 0)])
    north_side = padded[..., 2:, :]
    south_side = padded[..., :-2, :]
    upper_side = jnp.roll(centre, -1, axis=-1)
    lower_side = jnp.roll(centre, 1, axis=-1)
    laplace = east_side + west_side + north_side + south_side + upper_side + lower_side - 6.0 * centre
    result = velocity[:, None] * (0.5 * (east_side - west_side)) + viscosity * laplace
    coupling = shear_rate[:, None] * centre[..., 0:1, :, :, :]
    nothing = jnp.zeros_like(coupling)
    return result - jnp.concatenate([nothing, coupling, nothing], axis=-4)

def wrapped(field):
    return jnp.concatenate([field[:, -1:], field, field[:, :1]], axis=1)

def advance(field, velocity, shear_rate):
    first = operate_rim(wrapped(field), velocity, shear_rate)
    predicted = field + time_step * first
    second = operate_rim(wrapped(predicted), velocity, shear_rate)
    return field + 0.5 * time_step * (first + second)

def reference(adjoint_init, forward_snaps, base_speed, fwd_times, adj_times, horizon):
    padded_speed = jnp.pad(base_speed, 1)
    shear_rate = 0.5 * (padded_speed[2:] - padded_speed[:-2])
    forward_flat = forward_snaps.reshape(forward_snaps.shape[0], -1)
    scale = 1.0 / math.sqrt(3 * NX * NY * NZ)

    def one_run(field):
        collected = []
        for step_index in range(SNAP):
            field = advance(field, base_speed, shear_rate)
            snapshot = field.astype(jnp.bfloat16).reshape(1, -1)
            collected.append(lax.dot_general(snapshot, forward_flat, (((1,), (1,)), ((), ())), preferred_element_type=jnp.float32))
        return (field, jnp.concatenate(collected, 0))
    finals, sums = lax.map(one_run, adjoint_init)
    inside = adj_times[:, :, None] + fwd_times[None, None, :] <= horizon[:, None, None]
    hankel = jnp.where(inside, sums * scale, jnp.zeros_like(sums))
    return (finals, hankel)
```

```python
import functools
import math

import jax
import jax.numpy as jnp
from jax import lax
from jax.experimental import pallas as pl
from jax.experimental.pallas import tpu as pltpu
from jax.sharding import PartitionSpec as P

SNAP = 4
time_step = 0.5
viscosity = 0.2

ROWS = 16
PAD = 8


def stencil(src, i, rows, east, west, lanes):
    row0 = rows
    centre = [src[i, h, pl.ds(row0, ROWS), :] for h in (0, 1)]
    up = [pltpu.roll(c, 127, 1) for c in centre]
    down = [pltpu.roll(c, 1, 1) for c in centre]
    out = []
    for h in (0, 1):
        above = jnp.where(lanes == 127, up[1 - h], up[h])
        below = jnp.where(lanes == 0, down[1 - h], down[h])
        north = src[i, h, pl.ds(row0 + 1, ROWS), :]
        south = src[i, h, pl.ds(row0 - 1, ROWS), :]
        around = (north + south) + (above + below)
        value = east * src[i + 1, h, pl.ds(row0, ROWS), :] + west * src[i - 1, h, pl.ds(row0, ROWS), :]
        value = value + (time_step * viscosity) * around + (1.0 - 6.0 * time_step * viscosity) * centre[h]
        out.append(value)
    return out


def evolve_kernel(*refs, coupled, keep, planes, ny):
    refs = list(refs)
    odd = refs.pop(0)
    east_ref, west_ref = refs.pop(0), refs.pop(0)
    shear_ref = refs.pop(0) if coupled else None
    own, swapped, shifted = refs.pop(0), refs.pop(0), refs.pop(0)
    others = [refs.pop(0) for _ in range(4)] if coupled else [None] * 4
    new, snaps = refs.pop(0), refs.pop(0)
    work = [refs.pop(0) for _ in range(4)]
    steps = ny // ROWS
    n = planes
    is_odd = odd[0]
    swap_at = jnp.where(is_odd == 1, 0, 2 * n)
    shift_at = 2 * n - swap_at
    lanes = lax.broadcasted_iota(jnp.int32, (ROWS, 128), 1)
    zeros = jnp.zeros((PAD, 128), jnp.float32)
    for buffer in work:
        for i in range(buffer.shape[0]):
            for h in (0, 1):
                buffer[i, h, pl.ds(0, PAD), :] = zeros
                buffer[i, h, pl.ds(PAD + ny, PAD), :] = zeros

    def fill(t, _):
        row0 = pl.multiple_of(t * ROWS, ROWS)
        for i in range(n):
            for h in (0, 1):
                cols = pl.ds(h * 128, 128)
                rows = pl.ds(PAD + row0, ROWS)
                work[0][n + i, h, rows, :] = own[i, pl.ds(row0, ROWS), cols]
                work[0][swap_at + i, h, rows, :] = swapped[i, pl.ds(row0, ROWS), cols].astype(jnp.float32)
                work[0][shift_at + i, h, rows, :] = shifted[i, pl.ds(row0, ROWS), cols].astype(jnp.float32)
        return 0

    lax.fori_loop(0, steps, fill, 0)

    for k in range(4):
        src = work[k]
        dst = work[k + 1] if k < 3 else None

        def apply(t, _, k=k, src=src, dst=dst):
            row0 = pl.multiple_of(t * ROWS, ROWS)
            at = PAD + row0
            east = east_ref[pl.ds(row0, ROWS), :]
            west = west_ref[pl.ds(row0, ROWS), :]
            for i in range(k + 1, 3 * n - 1 - k):
                value = stencil(src, i - k, at, east, west, lanes)
                for h in (0, 1):
                    cols = pl.ds(h * 128, 128)
                    rows = pl.ds(at, ROWS)
                    got = value[h]
                    if coupled:
                        got = got - shear_ref[pl.ds(row0, ROWS), :] * others[k][i - k, h, rows, :]
                    if k % 2 == 1:
                        got = 0.5 * (work[k - 1][i - k + 1, h, rows, :] + got)
                    if dst is not None:
                        dst[i - k - 1, h, rows, :] = got
                    if k % 2 == 1 and n <= i < 2 * n:
                        snaps[k // 2, i - n, pl.ds(row0, ROWS), cols] = got.astype(jnp.bfloat16)
                    if k == 3:
                        new[i - n, pl.ds(row0, ROWS), cols] = got
            return 0

        lax.fori_loop(0, steps, apply, 0)


def evolve(odd, coefficients, own, swapped, shifted, others=None, keep=False):
    planes, ny, nz = own.shape
    coupled = others is not None
    vmem = pl.BlockSpec(memory_space=pltpu.VMEM)
    kept = [jax.ShapeDtypeStruct((3 * planes - 2 * k, 2, ny + 2 * PAD, 128), jnp.float32) for k in range(4)]
    outs = [jax.ShapeDtypeStruct(own.shape, jnp.float32), jax.ShapeDtypeStruct((2,) + own.shape, jnp.bfloat16)]
    scratch = [] if keep else [pltpu.VMEM(s.shape, s.dtype) for s in kept]
    outs = outs + (kept if keep else [])
    args = [odd, coefficients[0], coefficients[1]] + ([coefficients[2]] if coupled else []) + [own, swapped, shifted]
    args = args + (list(others) if coupled else [])
    return pl.pallas_call(
        functools.partial(evolve_kernel, coupled=coupled, keep=keep, planes=planes, ny=ny),
        out_shape=outs,
        in_specs=[pl.BlockSpec(memory_space=pltpu.SMEM)] + [vmem] * (len(args) - 1),
        out_specs=[vmem] * len(outs),
        scratch_shapes=scratch,
        compiler_params=pltpu.CompilerParams(vmem_limit_bytes=28 * 1024 * 1024),
        name="evolve_v" if coupled else ("evolve_u" if keep else "evolve_w"),
    )(*args)


def inner_kernel(run, snaps, *refs, pieces, ny):
    *fields, out = refs
    pairs = [(k, s) for k in range(pieces) for s in range(fields[0].shape[0])]

    @pl.when(pl.program_id(0) == 0)
    def _():
        out[...] = jnp.zeros_like(out)

    def body(t, sums):
        sums = list(sums)
        rows = pl.ds(pl.multiple_of(t * ROWS, ROWS), ROWS)
        for h in (0, 1):
            cols = pl.ds(h * 128, 128)
            mine = [snaps[j, 0, rows, cols].astype(jnp.float32) for j in (0, 1)]
            for p, (k, s) in enumerate(pairs):
                ref = fields[k]
                theirs = ref[s, 0, rows, cols].astype(jnp.float32)
                for j in (0, 1):
                    both = mine[j] * theirs
                    sums[j * len(pairs) + p] = sums[j * len(pairs) + p] + (both[:8] + both[8:])
        return tuple(sums)

    zero = jnp.zeros((8, 128), jnp.float32)
    sums = lax.fori_loop(0, ny // ROWS, body, tuple(zero for _ in range(2 * len(pairs))))
    per = len(pairs) // pieces
    for j in (0, 1):
        for p, (k, s) in enumerate(pairs):
            out[j, (run[0] ^ k) * per + s] += sums[j * len(pairs) + p]


def inner(run, snaps, fields):
    _, planes, ny, nz = snaps.shape
    count = fields[0].shape[0]
    specs = [pl.BlockSpec(memory_space=pltpu.SMEM), pl.BlockSpec((2, 1, ny, nz), lambda i: (0, i, 0, 0))]
    specs += [pl.BlockSpec((count, 1, ny, nz), lambda i: (0, i, 0, 0)) for _ in fields]
    return pl.pallas_call(
        functools.partial(inner_kernel, pieces=len(fields), ny=ny),
        grid=(planes,),
        out_shape=jax.ShapeDtypeStruct((2, count * len(fields), 8, 128), jnp.float32),
        in_specs=specs,
        out_specs=pl.BlockSpec((2, count * len(fields), 8, 128), lambda i: (0, 0, 0, 0)),
        compiler_params=pltpu.CompilerParams(vmem_limit_bytes=12 * 1024 * 1024),
        name="inner",
    )(run, snaps, *fields)


def permute(array, axis, target):
    size = lax.axis_size(axis)
    return lax.ppermute(array, axis, [(i, target(i, size)) for i in range(size)])


def swap(array):
    return permute(array, "space", lambda i, n: i ^ 1)


def shift(array):
    return permute(array, "space", lambda i, n: (i + 2 - 4 * (i % 2)) % n)


def gather(field, runs):
    got = [field]
    for bit in range(int(math.log2(runs)) - 1, -1, -1):
        far = 1 << bit
        got = got + [permute(g, "run", lambda i, n: i ^ far) for g in got]
    return got


def on_device(adjoint_init, forward_snaps, base_speed, fwd_times, adj_times, horizon):
    runs, spaces = lax.axis_size("run"), lax.axis_size("space")
    _, parts, planes, ny, nz = adjoint_init.shape
    padded_speed = jnp.pad(base_speed, 1)
    shear_rate = 0.5 * (padded_speed[2:] - padded_speed[:-2])
    half = time_step * 0.5 * base_speed
    wide = lambda a: jnp.broadcast_to(a[:, None], (ny, 128))
    coefficients = (
        wide(half + time_step * viscosity),
        wide(time_step * viscosity - half),
        wide(time_step * shear_rate),
    )
    run = lax.axis_index("run").astype(jnp.int32)[None]
    odd = (lax.axis_index("space") % 2).astype(jnp.int32)[None]

    fields = []
    order = [r for r in range(runs)]
    for c in range(parts):
        near = forward_snaps[:, c]
        fields.append(gather(near, runs))
    index = [0]
    for bit in range(int(math.log2(runs)) - 1, -1, -1):
        index = index + [k ^ (1 << bit) for k in index]
    fields = [[f[index.index(k)] for k in order] for f in fields]

    current = [adjoint_init[0, c] for c in range(parts)]
    sent = [q.astype(jnp.bfloat16) for q in current]
    sums = []
    for phase in range(SNAP // 2):
        swapped = [swap(s) for s in sent]
        shifted = [shift(s) for s in swapped]
        total = None
        kept = None
        for c in range(parts):
            others = kept if c == 1 else None
            result = evolve(odd, coefficients, current[c], swapped[c], shifted[c], others, keep=(c == 0))
            current[c], snaps = result[0], result[1]
            if c == 0:
                kept = result[2:]
            sent[c] = snaps[1]
            part = inner(run, snaps, fields[c])
            total = part if total is None else total + part
        sums.append(total)
    columns = jnp.stack(sums).reshape(SNAP, -1, 8, 128).sum(2)
    bit = 1
    while bit < spaces:
        columns = columns + permute(columns, "space", lambda i, n: i ^ bit)
        bit *= 2
    summed = columns.sum(-1)[None]
    scale = 1.0 / math.sqrt(parts * planes * spaces * ny * nz)
    inside = adj_times[:, :, None] + fwd_times[None, None, :] <= horizon[:, None, None]
    hankel = jnp.where(inside, summed * scale, jnp.zeros_like(summed))
    return (jnp.stack(current)[None], hankel)


def solution(mesh):
    in_specs = (
        P("run", None, "space", None, None),
        P("run", None, "space", None, None),
        P(),
        P(),
        P("run", None),
        P("run"),
    )
    out_specs = (P("run", None, "space", None, None), P("run", None, None))
    return jax.shard_map(
        on_device, mesh=mesh, in_specs=in_specs, out_specs=out_specs, check_vma=False
    )
```

```python
import functools
import math

import jax
import jax.numpy as jnp
from jax import lax
from jax.experimental import pallas as pl
from jax.experimental.pallas import tpu as pltpu
from jax.sharding import PartitionSpec as P

SNAP = 4
time_step = 0.5
viscosity = 0.2


ROWS = 16
PAD = 8
UNROLL = 6


def in_hbm(array):
    return pltpu.with_memory_space_constraint(array, pltpu.HBM)


def in_vmem(array):
    return pltpu.with_memory_space_constraint(array, pltpu.VMEM)


def cost(us):
    return pl.CostEstimate(flops=0, transcendentals=0, bytes_accessed=int(us * 3.0e6))


def stencil(src, i, rows, east, west, lanes):
    row0 = rows
    centre = [src[i, h, pl.ds(row0, ROWS), :] for h in (0, 1)]
    up = [pltpu.roll(c, 127, 1) for c in centre]
    down = [pltpu.roll(c, 1, 1) for c in centre]
    out = []
    for h in (0, 1):
        above = jnp.where(lanes == 127, up[1 - h], up[h])
        below = jnp.where(lanes == 0, down[1 - h], down[h])
        north = src[i, h, pl.ds(row0 + 1, ROWS), :]
        south = src[i, h, pl.ds(row0 - 1, ROWS), :]
        around = (north + south) + (above + below)
        value = east * src[i + 1, h, pl.ds(row0, ROWS), :] + west * src[i - 1, h, pl.ds(row0, ROWS), :]
        value = value + (time_step * viscosity) * around + (1.0 - 6.0 * time_step * viscosity) * centre[h]
        out.append(value)
    return out


def evolve_kernel(*refs, coupled, keep, planes, ny, at):
    refs = list(refs)
    odd = refs.pop(0)
    coefficients = refs.pop(0)
    east_ref, west_ref, shear_ref = coefficients.at[0], coefficients.at[1], coefficients.at[2]
    own, swapped, shifted = refs.pop(0), refs.pop(0), refs.pop(0)
    others = [refs.pop(0) for _ in range(4)] if coupled else [None] * 4
    new, snaps = refs.pop(0), [refs.pop(0), refs.pop(0)]
    work = [refs.pop(0) for _ in range(4)]
    sems = refs.pop(0)
    steps = ny // ROWS
    n = planes
    copies = []
    for i in range(n):
        for h in (0, 1):
            source = own.at[(*at, i, slice(None), pl.ds(h * 128, 128))]
            copies.append(pltpu.make_async_copy(source, work[0].at[n + i, h, pl.ds(PAD, ny), :], sems.at[2 * i + h]))
    for copy in copies:
        copy.start()
    swap_at = jnp.where(odd[0] == 1, 0, 2 * n)
    shift_at = 2 * n - swap_at
    lanes = lax.broadcasted_iota(jnp.int32, (ROWS, 128), 1)
    zeros = jnp.zeros((PAD, 128), jnp.float32)
    for buffer in work:
        for i in range(buffer.shape[0]):
            for h in (0, 1):
                buffer[i, h, pl.ds(0, PAD), :] = zeros
                buffer[i, h, pl.ds(PAD + ny, PAD), :] = zeros

    def fill(t, _):
        row0 = pl.multiple_of(t * ROWS, ROWS)
        for i in range(n):
            for h in (0, 1):
                cols = pl.ds(h * 128, 128)
                rows = pl.ds(PAD + row0, ROWS)
                work[0][swap_at + i, h, rows, :] = swapped[i, pl.ds(row0, ROWS), cols].astype(jnp.float32)
                work[0][shift_at + i, h, rows, :] = shifted[i, pl.ds(row0, ROWS), cols].astype(jnp.float32)
        return 0

    lax.fori_loop(0, steps, fill, 0, unroll=UNROLL)
    for copy in copies:
        copy.wait()

    for k in range(4):
        src = work[k]
        dst = work[k + 1] if k < 3 else None

        def apply(t, _, k=k, src=src, dst=dst):
            row0 = pl.multiple_of(t * ROWS, ROWS)
            east = east_ref[pl.ds(row0, ROWS), :]
            west = west_ref[pl.ds(row0, ROWS), :]
            for i in range(k + 1, 3 * n - 1 - k):
                value = stencil(src, i - k, PAD + row0, east, west, lanes)
                for h in (0, 1):
                    cols = pl.ds(h * 128, 128)
                    rows = pl.ds(PAD + row0, ROWS)
                    got = value[h]
                    if coupled:
                        got = got - shear_ref[pl.ds(row0, ROWS), :] * others[k][i - k, h, rows, :]
                    if k % 2 == 1:
                        got = 0.5 * (work[k - 1][i - k + 1, h, rows, :] + got)
                    if dst is not None:
                        dst[i - k - 1, h, rows, :] = got
                    if k % 2 == 1 and n <= i < 2 * n:
                        snaps[k // 2][i - n, pl.ds(row0, ROWS), cols] = got.astype(jnp.bfloat16)
                    if k == 3:
                        new[i - n, pl.ds(row0, ROWS), cols] = got
            return 0

        lax.fori_loop(0, steps, apply, 0, unroll=UNROLL)


def evolve(odd, coefficients, own, at, swapped, shifted, others=None, keep=False):
    planes, ny, nz = swapped.shape
    coupled = others is not None
    vmem = pl.BlockSpec(memory_space=pltpu.VMEM)
    kept = [jax.ShapeDtypeStruct((3 * planes - 2 * k, 2, ny + 2 * PAD, 128), jnp.float32) for k in range(4)]
    first = len(at) > 0
    new = (pltpu.VMEM if first else jax.ShapeDtypeStruct)((planes, ny, nz), jnp.float32)
    work = [pltpu.VMEM(s.shape, s.dtype) for s in kept]
    scratch = [] if keep else work
    outs = [new] + [pltpu.VMEM((planes, ny, nz), jnp.bfloat16)] * 2 + (work if keep else [])
    before = [coefficients]
    after = [in_vmem(a) for a in (swapped, shifted) + (tuple(others) if coupled else ())]
    own = in_hbm(own) if first else in_vmem(own)
    return pl.pallas_call(
        functools.partial(evolve_kernel, coupled=coupled, keep=keep, planes=planes, ny=ny, at=at),
        out_shape=outs,
        in_specs=[pl.BlockSpec(memory_space=pltpu.SMEM)]
        + [vmem] * len(before)
        + [pl.BlockSpec(memory_space=pltpu.HBM) if first else vmem]
        + [vmem] * len(after),
        out_specs=[vmem] * len(outs),
        scratch_shapes=scratch + [pltpu.SemaphoreType.DMA((2 * planes,))],
        compiler_params=pltpu.CompilerParams(vmem_limit_bytes=12 * 1024 * 1024),
        cost_estimate=cost(4.5),
        name="evolve_v" if coupled else ("evolve_u" if keep else "evolve_w"),
    )(odd, *before, own, *after)


def round_kernel(fields, after, out, buffer, sems, *, c):
    copies = [pltpu.make_async_copy(fields.at[0, c, i], buffer.at[i], sems.at[i]) for i in range(out.shape[0])]
    for copy in copies:
        copy.start()
    for i, copy in enumerate(copies):
        copy.wait()
        out[i] = buffer[i].astype(jnp.bfloat16)


def rounded(fields, c, after):
    _, _, planes, ny, nz = fields.shape
    return pl.pallas_call(
        functools.partial(round_kernel, c=c),
        out_shape=pltpu.VMEM((planes, ny, nz), jnp.bfloat16),
        in_specs=[pl.BlockSpec(memory_space=pltpu.HBM), pl.BlockSpec(memory_space=pl.ANY)],
        out_specs=pl.BlockSpec(memory_space=pltpu.VMEM),
        scratch_shapes=[pltpu.VMEM((planes, ny, nz), jnp.float32), pltpu.SemaphoreType.DMA((planes,))],
        compiler_params=pltpu.CompilerParams(vmem_limit_bytes=2 * 1024 * 1024),
        cost_estimate=cost(1),
        name="rounded",
    )(in_hbm(fields), after)


def inner_kernel(run, *refs, ny, at):
    *refs, out, buffer, sems = refs
    snaps, fields = refs[:2], refs[2:]
    planes = snaps[0].shape[0]
    pieces, count = buffer.shape[0], buffer.shape[1]
    pairs = [(k, s) for k in range(pieces) for s in range(count)]
    copies = []
    for i in range(planes):
        for k in range(pieces):
            source = fields[k].at[(slice(None), *at[k], i)]
            copies.append(pltpu.make_async_copy(source, buffer.at[k, :, i], sems.at[i * pieces + k]))
    for copy in copies:
        copy.start()
    sums = tuple(jnp.zeros((8, 128), jnp.float32) for _ in range(2 * len(pairs)))
    for i in range(planes):
        for copy in copies[i * pieces : (i + 1) * pieces]:
            copy.wait()

        def body(t, sums, i=i):
            sums = list(sums)
            rows = pl.ds(pl.multiple_of(t * ROWS, ROWS), ROWS)
            for h in (0, 1):
                cols = pl.ds(h * 128, 128)
                mine = [snaps[j][i, rows, cols].astype(jnp.float32) for j in (0, 1)]
                for p, (k, s) in enumerate(pairs):
                    theirs = buffer[k, s, i, rows, cols].astype(jnp.float32)
                    for j in (0, 1):
                        both = mine[j] * theirs
                        sums[j * len(pairs) + p] = sums[j * len(pairs) + p] + (both[:8] + both[8:])
            return tuple(sums)

        sums = lax.fori_loop(0, ny // ROWS, body, sums, unroll=4)
    for j in (0, 1):
        for p, (k, s) in enumerate(pairs):
            out[j, (run[0] ^ k) * count + s] = sums[j * len(pairs) + p]


def inner(run, snaps, fields, at):
    planes, ny, nz = snaps[0].shape
    vmem, hbm = pl.BlockSpec(memory_space=pltpu.VMEM), pl.BlockSpec(memory_space=pltpu.HBM)
    count, pieces = fields[0].shape[0], len(fields)
    return pl.pallas_call(
        functools.partial(inner_kernel, ny=ny, at=at),
        out_shape=jax.ShapeDtypeStruct((2, count * pieces, 8, 128), jnp.float32),
        in_specs=[pl.BlockSpec(memory_space=pltpu.SMEM)] + [vmem] * 2 + [hbm] * pieces,
        out_specs=vmem,
        scratch_shapes=[
            pltpu.VMEM((pieces, count, planes, ny, nz), fields[0].dtype),
            pltpu.SemaphoreType.DMA((planes * pieces,)),
        ],
        compiler_params=pltpu.CompilerParams(vmem_limit_bytes=6 * 1024 * 1024),
        cost_estimate=cost(2),
        name="inner",
    )(run, *[in_vmem(a) for a in snaps], *[in_hbm(f) for f in fields])


def permute(array, axis, target):
    size = lax.axis_size(axis)
    return lax.ppermute(array, axis, [(i, target(i, size)) for i in range(size)])


def swap(array):
    return permute(array, "space", lambda i, n: i ^ 1)


def shift(array):
    return permute(array, "space", lambda i, n: (i + 2 - 4 * (i % 2)) % n)


def gather(snaps, c, near, runs):
    got, at = list(near), [(c,)] * len(near)
    half = runs // 2
    got.append(permute(snaps[:, c], "run", lambda i, n: i ^ half))
    bit = half // 2
    base = {half: got[-1]}
    while bit > 0:
        for k in list(base):
            base[k ^ bit] = permute(base[k], "run", lambda i, n: i ^ bit)
        bit //= 2
    return got[:half] + [base[k] for k in range(half, runs)], at + [()] * (runs - half)


def gather_near(snaps, runs):
    got = {0: snaps}
    bit = runs // 4
    while bit > 0:
        for k in list(got):
            got[k ^ bit] = permute(got[k], "run", lambda i, n: i ^ bit)
        bit //= 2
    return [got[k] for k in range(runs // 2)]


def on_device(adjoint_init, forward_snaps, base_speed, fwd_times, adj_times, horizon):
    runs, spaces = lax.axis_size("run"), lax.axis_size("space")
    _, parts, planes, ny, nz = adjoint_init.shape
    padded_speed = jnp.pad(base_speed, 1)
    shear_rate = 0.5 * (padded_speed[2:] - padded_speed[:-2])
    half = time_step * 0.5 * base_speed
    rows = jnp.stack([half + time_step * viscosity, time_step * viscosity - half, time_step * shear_rate])
    coefficients = jnp.broadcast_to(rows[:, :, None], (3, ny, 128))
    run = lax.axis_index("run").astype(jnp.int32)[None]
    odd = (lax.axis_index("space") % 2).astype(jnp.int32)[None]

    current = [(adjoint_init, (0, c)) for c in range(parts)]
    sent = []
    for c in range(parts):
        sent.append(rounded(adjoint_init, c, coefficients))
    fields, sums = [], [None] * (SNAP // 2)
    swapped, shifted = {}, {}
    for c in range(parts):
        swapped[0, c] = swap(sent[c])
    near = gather_near(forward_snaps, runs)
    for c in range(parts):
        fields.append(gather(forward_snaps, c, near, runs))
    for phase in range(SNAP // 2):
        kept = None
        for c in range(parts):
            if phase > 0:
                swapped[phase, c] = swap(sent[c])
            shifted[phase, c] = shift(swapped[phase, c])
            others = kept if c == 1 else None
            result = evolve(odd, coefficients, *current[c], swapped[phase, c], shifted[phase, c], others, keep=(c == 0))
            current[c], snaps = (result[0], ()), result[1:3]
            if c == 0:
                kept = result[3:]
            sent[c] = snaps[1]
            part = inner(run, snaps, *fields[c])
            sums[phase] = part if c == 0 else sums[phase] + part
    columns = jnp.stack(sums).reshape(SNAP, -1, 8, 128).sum(2)
    bit = 1
    while bit < spaces:
        columns = columns + permute(columns, "space", lambda i, n: i ^ bit)
        bit *= 2
    summed = columns.sum(-1)[None]
    scale = 1.0 / math.sqrt(parts * planes * spaces * ny * nz)
    inside = adj_times[:, :, None] + fwd_times[None, None, :] <= horizon[:, None, None]
    hankel = jnp.where(inside, summed * scale, jnp.zeros_like(summed))
    return (jnp.stack([q for q, _ in current])[None], hankel)


def solution(mesh):
    in_specs = (
        P("run", None, "space", None, None),
        P("run", None, "space", None, None),
        P(),
        P(),
        P("run", None),
        P("run"),
    )
    out_specs = (P("run", None, "space", None, None), P("run", None, None))
    return jax.shard_map(
        on_device, mesh=mesh, in_specs=in_specs, out_specs=out_specs, check_vma=False
    )
```

```python
import functools
import math

import jax
import jax.numpy as jnp
from jax import lax
from jax.experimental import pallas as pl
from jax.experimental.pallas import tpu as pltpu
from jax.sharding import PartitionSpec as P

SNAP = 4
time_step = 0.5
viscosity = 0.2


PAD = 8
TILE = 16


def in_hbm(array):
    return pltpu.with_memory_space_constraint(array, pltpu.HBM)


def in_vmem(array):
    return pltpu.with_memory_space_constraint(array, pltpu.VMEM)


def cost(us):
    return pl.CostEstimate(flops=0, transcendentals=0, bytes_accessed=int(us * 3.0e6))


def evolve_kernel(*refs, coupled, planes, ny, at, pieces, split):
    refs = list(refs)
    coefficients, around_z = refs.pop(0), refs.pop(0)
    own = refs.pop(0)
    swapped, shifted = [refs.pop(0) for _ in range(pieces)], [refs.pop(0) for _ in range(pieces)]
    others = [refs.pop(0) for _ in range(4)] if coupled else [None] * 4
    new, snaps = refs.pop(0), [[refs.pop(0)], [refs.pop(0) for _ in range(split)]]
    work = [refs.pop(0) for _ in range(4)]
    sems = refs.pop(0)
    n = planes
    halves = [(h, pl.ds(h * 128, 128)) for h in (0, 1)]
    rows = pl.ds(PAD, ny)
    copies = []
    for i in range(n):
        for h, cols in halves:
            source = own.at[(*at, i, slice(None), cols)]
            copies.append(pltpu.make_async_copy(source, work[0].at[n + i, h, rows, :], sems.at[2 * i + h]))
    for copy in copies:
        copy.start()
    swap_at = jnp.where(lax.axis_index("space") % 2 == 1, 0, 2 * n)
    shift_at = 2 * n - swap_at
    zeros = jnp.zeros((PAD, 128), jnp.float32)
    for buffer in work:
        for i in range(buffer.shape[0]):
            for h in (0, 1):
                buffer[i, h, pl.ds(0, PAD), :] = zeros
                buffer[i, h, pl.ds(PAD + ny, PAD), :] = zeros
    for i in range(n):
        for h, cols in halves:
            piece, place = i * pieces // n, i % (n // pieces)
            work[0][swap_at + i, h, rows, :] = swapped[piece][place, :, cols].astype(jnp.float32)
            work[0][shift_at + i, h, rows, :] = shifted[piece][place, :, cols].astype(jnp.float32)
    for copy in copies:
        copy.wait()

    weight = time_step * viscosity
    for k in range(4):
        src = work[k]
        second = k % 2
        count = 3 * n - 2 - 2 * k
        lines = [jnp.concatenate([src[j, h, rows, :] for h in (0, 1)], axis=1) for j in range(1, 1 + count)]
        lines = jnp.concatenate([line.astype(jnp.bfloat16) for line in lines], axis=0)
        beside = jnp.dot(lines, around_z[...], preferred_element_type=jnp.float32)
        east, west, shear = coefficients[3 * second], coefficients[3 * second + 1], coefficients[3 * second + 2]
        for j in range(1, 1 + count):
            i = j + k
            for h, cols in halves:
                around = src[j, h, pl.ds(PAD + 1, ny), :] + src[j, h, pl.ds(PAD - 1, ny), :]
                around = around + beside[(j - 1) * ny : j * ny, h * 128 : (h + 1) * 128]
                centre = src[j, h, rows, :]
                if second:
                    got = (weight * weight) * around + (weight * (1.0 - 6.0 * weight)) * centre
                else:
                    got = around + ((1.0 - 6.0 * weight) / weight) * centre
                got = got + (east * src[j + 1, h, rows, :] + west * src[j - 1, h, rows, :])
                if coupled:
                    got = got - shear * others[k][j, h, rows, :]
                if second:
                    got = work[k - 1][j + 1, h, rows, :] + got
                if k < 3:
                    work[k + 1][j - 1, h, rows, :] = got
                if second and n <= i < 2 * n:
                    scaled = (0.5 if k == 1 else 0.25) * got
                    into = snaps[k // 2]
                    into[(i - n) * len(into) // n][i % (n // len(into)), :, cols] = scaled.astype(jnp.bfloat16)
                    if k == 3:
                        new[i - n, :, cols] = scaled


def evolve(coefficients, around_z, own, at, swapped, shifted, others=None, keep=False, split=1):
    pieces = len(swapped)
    planes, ny, nz = swapped[0].shape
    planes *= pieces
    coupled = others is not None
    vmem = pl.BlockSpec(memory_space=pltpu.VMEM)
    kept = [jax.ShapeDtypeStruct((3 * planes - 2 * k, 2, ny + 2 * PAD, 128), jnp.float32) for k in range(4)]
    first = len(at) > 0
    new = (pltpu.VMEM if first else jax.ShapeDtypeStruct)((planes, ny, nz), jnp.float32)
    work = [pltpu.VMEM(s.shape, s.dtype) for s in kept]
    scratch = [] if keep else work
    outs = [new] + [pltpu.VMEM((planes // k, ny, nz), jnp.bfloat16) for k in [1] + [split] * split] + (work if keep else [])
    before = [coefficients, around_z]
    after = [in_vmem(a) for a in swapped + shifted + (tuple(others) if coupled else ())]
    own = in_hbm(own) if first else in_vmem(own)
    return pl.pallas_call(
        functools.partial(evolve_kernel, coupled=coupled, planes=planes, ny=ny, at=at, pieces=pieces, split=split),
        out_shape=outs,
        in_specs=[vmem] * len(before)
        + [pl.BlockSpec(memory_space=pltpu.HBM) if first else vmem]
        + [vmem] * len(after),
        out_specs=[vmem] * len(outs),
        scratch_shapes=scratch + [pltpu.SemaphoreType.DMA((2 * planes,))],
        compiler_params=pltpu.CompilerParams(vmem_limit_bytes=12 * 1024 * 1024),
        cost_estimate=cost(4.5),
        name="evolve_v" if coupled else ("evolve_u" if keep else "evolve_w"),
    )(*before, own, *after)


def round_kernel(fields, snaps, *refs, c):
    *outs, chunk, buffer, sems, chunk_sems = refs
    planes = buffer.shape[0]
    copies = [pltpu.make_async_copy(fields.at[0, c, i], buffer.at[i], sems.at[i]) for i in range(planes)]
    slices = [pltpu.make_async_copy(snaps.at[s, c], chunk.at[s], chunk_sems.at[s]) for s in range(chunk.shape[0])]
    for copy in copies + slices:
        copy.start()
    for i, copy in enumerate(copies):
        copy.wait()
        outs[i * len(outs) // planes][i % (planes // len(outs))] = buffer[i].astype(jnp.bfloat16)
    for copy in slices:
        copy.wait()


def rounded(fields, snaps, c):
    _, _, planes, ny, nz = fields.shape
    count = snaps.shape[0]
    vmem, hbm = pl.BlockSpec(memory_space=pltpu.VMEM), pl.BlockSpec(memory_space=pltpu.HBM)
    half = pltpu.VMEM((planes // 2, ny, nz), jnp.bfloat16)
    return pl.pallas_call(
        functools.partial(round_kernel, c=c),
        out_shape=[half, half, pltpu.VMEM((count, planes, ny, nz), snaps.dtype)],
        in_specs=[hbm, hbm],
        out_specs=[vmem] * 3,
        scratch_shapes=[
            pltpu.VMEM((planes, ny, nz), jnp.float32),
            pltpu.SemaphoreType.DMA((planes,)),
            pltpu.SemaphoreType.DMA((count,)),
        ],
        compiler_params=pltpu.CompilerParams(vmem_limit_bytes=2 * 1024 * 1024),
        cost_estimate=cost(1),
        name="rounded",
    )(in_hbm(fields), in_hbm(snaps))


def prepare_kernel(fields, snaps, speed, *refs, planes, ny, nz):
    parts = fields.shape[1]
    outs, chunks = refs[: parts - 1], refs[parts - 1 : 2 * parts - 2]
    coefficients, around_z, buffer, padded, sems, chunk_sems = refs[2 * parts - 2 :]
    copies = []
    for c in range(1, parts):
        for i in range(planes):
            at = (c - 1) * planes + i
            copies.append(pltpu.make_async_copy(fields.at[0, c, i], buffer.at[c - 1, i], sems.at[at]))
    count = snaps.shape[0]
    slices = [
        pltpu.make_async_copy(snaps.at[s, c], chunks[c - 1].at[s], chunk_sems.at[(c - 1) * count + s])
        for c in range(1, parts)
        for s in range(count)
    ]
    for copy in copies + slices:
        copy.start()
    base = jnp.broadcast_to(speed[...], (128, ny)).T
    padded[pl.ds(0, PAD), :] = jnp.zeros((PAD, 128), jnp.float32)
    padded[pl.ds(PAD + ny, PAD), :] = jnp.zeros((PAD, 128), jnp.float32)
    padded[pl.ds(PAD, ny), :] = base
    shear = (0.5 * time_step) * (padded[pl.ds(PAD + 1, ny), :] - padded[pl.ds(PAD - 1, ny), :])
    weight = time_step * viscosity
    half = (0.5 * time_step) * base
    for k, scale in enumerate((1.0 / weight, weight)):
        coefficients[3 * k] = scale * (half + weight)
        coefficients[3 * k + 1] = scale * (weight - half)
        coefficients[3 * k + 2] = scale * shear
    apart = lax.broadcasted_iota(jnp.int32, (nz, nz), 0) - lax.broadcasted_iota(jnp.int32, (nz, nz), 1)
    apart = jnp.abs(apart)
    around_z[...] = jnp.where((apart == 1) | (apart == nz - 1), 1.0, 0.0).astype(jnp.bfloat16)
    for at, copy in enumerate(copies):
        copy.wait()
        c, i = at // planes, at % planes
        outs[c][i] = buffer[c, i].astype(jnp.bfloat16)
    for copy in slices:
        copy.wait()


def prepare(fields, snaps, speed):
    _, parts, planes, ny, nz = fields.shape
    count = snaps.shape[0]
    vmem, hbm = pl.BlockSpec(memory_space=pltpu.VMEM), pl.BlockSpec(memory_space=pltpu.HBM)
    outs = [pltpu.VMEM((planes, ny, nz), jnp.bfloat16)] * (parts - 1)
    outs += [pltpu.VMEM((count, planes, ny, nz), snaps.dtype)] * (parts - 1)
    outs += [pltpu.VMEM((6, ny, 128), jnp.float32), pltpu.VMEM((nz, nz), jnp.bfloat16)]
    got = pl.pallas_call(
        functools.partial(prepare_kernel, planes=planes, ny=ny, nz=nz),
        out_shape=outs,
        in_specs=[hbm, hbm, vmem],
        out_specs=[vmem] * len(outs),
        scratch_shapes=[
            pltpu.VMEM((parts - 1, planes, ny, nz), jnp.float32),
            pltpu.VMEM((ny + 2 * PAD, 128), jnp.float32),
            pltpu.SemaphoreType.DMA(((parts - 1) * planes,)),
            pltpu.SemaphoreType.DMA(((parts - 1) * count,)),
        ],
        compiler_params=pltpu.CompilerParams(vmem_limit_bytes=4 * 1024 * 1024),
        cost_estimate=cost(2),
        name="prepare",
    )(in_hbm(fields), in_hbm(snaps), speed[None])
    return got[: parts - 1], got[parts - 1 : 2 * parts - 2], got[-2], got[-1]


def inner_kernel(*refs, pieces, at):
    run = lax.axis_index("run")
    *refs, out = refs
    snaps, fields = [refs[0:1], refs[1 : 1 + pieces]], refs[1 + pieces :]
    count = fields[0].shape[0]
    planes, ny, _ = refs[0].shape
    pairs = [(k, s) for k in range(len(fields)) for s in range(count)]
    sums = tuple(jnp.zeros((8, 128), jnp.float32) for _ in range(2 * len(pairs)))
    for i in range(planes):

        def body(t, sums, i=i):
            sums = list(sums)
            rows = pl.ds(pl.multiple_of(t * TILE, TILE), TILE)
            for h in (0, 1):
                cols = pl.ds(h * 128, 128)
                mine = []
                for split in snaps:
                    piece, place = i * len(split) // planes, i % (planes // len(split))
                    mine.append(split[piece][place, rows, cols].astype(jnp.float32))
                for p, (k, s) in enumerate(pairs):
                    theirs = fields[k][(s, *at[k], i, rows, cols)].astype(jnp.float32)
                    for j in (0, 1):
                        both = mine[j] * theirs
                        sums[j * len(pairs) + p] = sums[j * len(pairs) + p] + (both[:8] + both[8:])
            return tuple(sums)

        sums = lax.fori_loop(0, ny // TILE, body, sums, unroll=4)
    for j in (0, 1):
        for p, (k, s) in enumerate(pairs):
            out[j, (run ^ k) * count + s] = sums[j * len(pairs) + p]


def inner(first, second, fields, at):
    vmem = pl.BlockSpec(memory_space=pltpu.VMEM)
    operands = [in_vmem(a) for a in (first, *second, *fields)]
    return pl.pallas_call(
        functools.partial(inner_kernel, pieces=len(second), at=at),
        out_shape=jax.ShapeDtypeStruct((2, fields[0].shape[0] * len(fields), 8, 128), jnp.float32),
        in_specs=[vmem] * len(operands),
        out_specs=vmem,
        compiler_params=pltpu.CompilerParams(vmem_limit_bytes=2 * 1024 * 1024),
        cost_estimate=cost(2),
        name="inner",
    )(*operands)


def permute(array, axis, target):
    size = lax.axis_size(axis)
    return lax.ppermute(array, axis, [(i, target(i, size)) for i in range(size)])


def each(arrays, target):
    got = []
    for array in arrays:
        got.append(permute(array, "space", target))
    return tuple(got)


def swap(arrays):
    return each(arrays, lambda i, n: i ^ 1)


def shift(arrays):
    return each(arrays, lambda i, n: (i + 2 - 4 * (i % 2)) % n)


def gather(chunk, c, near, runs):
    got, at = [chunk, *near[1:]], [()] + [(c,)] * (len(near) - 1)
    half = runs // 2
    got.append(permute(chunk, "run", lambda i, n: i ^ half))
    bit = half // 2
    base = {half: got[-1]}
    while bit > 0:
        for k in list(base):
            base[k ^ bit] = permute(base[k], "run", lambda i, n: i ^ bit)
        bit //= 2
    return got[:half] + [base[k] for k in range(half, runs)], at + [()] * (runs - half)


def gather_near(snaps, runs):
    got = {0: snaps}
    bit = runs // 4
    while bit > 0:
        for k in list(got):
            got[k ^ bit] = permute(got[k], "run", lambda i, n: i ^ bit)
        bit //= 2
    return [got[k] for k in range(runs // 2)]


def on_device(adjoint_init, forward_snaps, base_speed, fwd_times, adj_times, horizon):
    runs, spaces = lax.axis_size("run"), lax.axis_size("space")
    _, parts, planes, ny, nz = adjoint_init.shape
    current = [(adjoint_init, (0, c)) for c in range(parts)]
    *halves, chunk = rounded(adjoint_init, forward_snaps, 0)
    rest, chunks, coefficients, around_z = prepare(adjoint_init, forward_snaps, base_speed)
    sent = [tuple(halves)] + [(field,) for field in rest]
    chunks = [chunk, *chunks]
    fields, sums = [], [None] * (SNAP // 2)
    swapped, shifted = {}, {}
    for c in range(parts):
        swapped[0, c] = swap(sent[c])
    near = gather_near(forward_snaps, runs)
    for c in range(parts):
        fields.append(gather(chunks[c], c, near, runs))
    for phase in range(SNAP // 2):
        kept = None
        for c in range(parts):
            if phase > 0:
                swapped[phase, c] = swap(sent[c])
            shifted[phase, c] = shift(swapped[phase, c])
            others = kept if c == 1 else None
            split = 2 if (phase, c) == (SNAP // 2 - 2, parts - 1) else 1
            halos = swapped[phase, c], shifted[phase, c]
            result = evolve(coefficients, around_z, *current[c], *halos, others, keep=(c == 0), split=split)
            current[c], first = (result[0], ()), result[1]
            sent[c] = tuple(result[2 : 2 + split])
            if c == 0:
                kept = result[2 + split :]
            part = inner(first, sent[c], *fields[c])
            sums[phase] = part if c == 0 else sums[phase] + part
    columns = jnp.stack(sums).reshape(SNAP, -1, 8, 128).sum((2, 3))
    bit = 1
    while bit < spaces:
        columns = columns + permute(columns, "space", lambda i, n: i ^ bit)
        bit *= 2
    summed = columns[None]
    scale = 1.0 / math.sqrt(parts * planes * spaces * ny * nz)
    inside = adj_times[:, :, None] + fwd_times[None, None, :] <= horizon[:, None, None]
    hankel = jnp.where(inside, summed * scale, jnp.zeros_like(summed))
    return (jnp.stack([q for q, _ in current])[None], hankel)


def solution(mesh):
    in_specs = (
        P("run", None, "space", None, None),
        P("run", None, "space", None, None),
        P(),
        P(),
        P("run", None),
        P("run"),
    )
    out_specs = (P("run", None, "space", None, None), P("run", None, None))
    return jax.shard_map(
        on_device, mesh=mesh, in_specs=in_specs, out_specs=out_specs, check_vma=False
    )
```

```python
import functools
import math

import jax
import jax.numpy as jnp
from jax import lax
from jax.experimental import pallas as pl
from jax.experimental.pallas import tpu as pltpu
from jax.sharding import PartitionSpec as P

SNAP = 4
time_step = 0.5
viscosity = 0.2


PAD = 8
TILE = 16

SPLITS = {(0, 0): 2, (0, 1): 2, (0, 2): 2, (1, 0): 2, (1, 1): 2, (1, 2): 2}


def in_hbm(array):
    return pltpu.with_memory_space_constraint(array, pltpu.HBM)


def in_vmem(array):
    return pltpu.with_memory_space_constraint(array, pltpu.VMEM)


def cost(us):
    return pl.CostEstimate(flops=0, transcendentals=0, bytes_accessed=int(us * 3.0e6))


def evolve_kernel(*refs, coupled, planes, ny, at, pieces, split):
    refs = list(refs)
    coefficients, around_z = refs.pop(0), refs.pop(0)
    own = refs.pop(0)
    swapped, shifted = [refs.pop(0) for _ in range(pieces)], [refs.pop(0) for _ in range(pieces)]
    others = [refs.pop(0) for _ in range(4)] if coupled else [None] * 4
    new, snaps = refs.pop(0), [[refs.pop(0)], [refs.pop(0) for _ in range(split)]]
    work = [refs.pop(0) for _ in range(4)]
    sems = refs.pop(0)
    n = planes
    halves = [(h, pl.ds(h * 128, 128)) for h in (0, 1)]
    rows = pl.ds(PAD, ny)
    copies = []
    for i in range(n):
        for h, cols in halves:
            source = own.at[(*at, i, slice(None), cols)]
            copies.append(pltpu.make_async_copy(source, work[0].at[n + i, h, rows, :], sems.at[2 * i + h]))
    for copy in copies:
        copy.start()
    swap_at = jnp.where(lax.axis_index("space") % 2 == 1, 0, 2 * n)
    shift_at = 2 * n - swap_at
    zeros = jnp.zeros((PAD, 128), jnp.float32)
    for buffer in work:
        for i in range(buffer.shape[0]):
            for h in (0, 1):
                buffer[i, h, pl.ds(0, PAD), :] = zeros
                buffer[i, h, pl.ds(PAD + ny, PAD), :] = zeros
    for i in range(n):
        for h, cols in halves:
            piece, place = i * pieces // n, i % (n // pieces)
            work[0][swap_at + i, h, rows, :] = swapped[piece][place, :, cols].astype(jnp.float32)
            work[0][shift_at + i, h, rows, :] = shifted[piece][place, :, cols].astype(jnp.float32)
    for copy in copies:
        copy.wait()

    weight = time_step * viscosity
    for k in range(4):
        src = work[k]
        second = k % 2
        count = 3 * n - 2 - 2 * k
        lines = [jnp.concatenate([src[j, h, rows, :] for h in (0, 1)], axis=1) for j in range(1, 1 + count)]
        lines = jnp.concatenate([line.astype(jnp.bfloat16) for line in lines], axis=0)
        beside = jnp.dot(lines, around_z[...], preferred_element_type=jnp.float32)
        east, west, shear = coefficients[3 * second], coefficients[3 * second + 1], coefficients[3 * second + 2]
        for j in range(1, 1 + count):
            i = j + k
            for h, cols in halves:
                around = src[j, h, pl.ds(PAD + 1, ny), :] + src[j, h, pl.ds(PAD - 1, ny), :]
                around = around + beside[(j - 1) * ny : j * ny, h * 128 : (h + 1) * 128]
                centre = src[j, h, rows, :]
                if second:
                    got = (weight * weight) * around + (weight * (1.0 - 6.0 * weight)) * centre
                else:
                    got = around + ((1.0 - 6.0 * weight) / weight) * centre
                got = got + (east * src[j + 1, h, rows, :] + west * src[j - 1, h, rows, :])
                if coupled:
                    got = got - shear * others[k][j, h, rows, :]
                if second:
                    got = work[k - 1][j + 1, h, rows, :] + got
                if k < 3:
                    work[k + 1][j - 1, h, rows, :] = got
                if second and n <= i < 2 * n:
                    scaled = (0.5 if k == 1 else 0.25) * got
                    into = snaps[k // 2]
                    into[(i - n) * len(into) // n][i % (n // len(into)), :, cols] = scaled.astype(jnp.bfloat16)
                    if k == 3:
                        new[i - n, :, cols] = scaled


def evolve(coefficients, around_z, own, at, swapped, shifted, others=None, keep=False, split=1):
    pieces = len(swapped)
    planes, ny, nz = swapped[0].shape
    planes *= pieces
    coupled = others is not None
    vmem = pl.BlockSpec(memory_space=pltpu.VMEM)
    kept = [jax.ShapeDtypeStruct((3 * planes - 2 * k, 2, ny + 2 * PAD, 128), jnp.float32) for k in range(4)]
    first = len(at) > 0
    new = (pltpu.VMEM if first else jax.ShapeDtypeStruct)((planes, ny, nz), jnp.float32)
    work = [pltpu.VMEM(s.shape, s.dtype) for s in kept]
    scratch = [] if keep else work
    outs = [new] + [pltpu.VMEM((planes // k, ny, nz), jnp.bfloat16) for k in [1] + [split] * split] + (work if keep else [])
    before = [coefficients, around_z]
    after = [in_vmem(a) for a in swapped + shifted + (tuple(others) if coupled else ())]
    own = in_hbm(own) if first else in_vmem(own)
    return pl.pallas_call(
        functools.partial(evolve_kernel, coupled=coupled, planes=planes, ny=ny, at=at, pieces=pieces, split=split),
        out_shape=outs,
        in_specs=[vmem] * len(before)
        + [pl.BlockSpec(memory_space=pltpu.HBM) if first else vmem]
        + [vmem] * len(after),
        out_specs=[vmem] * len(outs),
        scratch_shapes=scratch + [pltpu.SemaphoreType.DMA((2 * planes,))],
        compiler_params=pltpu.CompilerParams(vmem_limit_bytes=12 * 1024 * 1024),
        cost_estimate=cost(4.5),
        name="evolve_v" if coupled else ("evolve_u" if keep else "evolve_w"),
    )(*before, own, *after)


def round_kernel(fields, out, buffer, sems):
    copies = [pltpu.make_async_copy(fields.at[0, 0, i], buffer.at[i], sems.at[i]) for i in range(buffer.shape[0])]
    for copy in copies:
        copy.start()
    for i, copy in enumerate(copies):
        copy.wait()
        out[i] = buffer[i].astype(jnp.bfloat16)


def rounded(fields, planes):
    ny, nz = fields.shape[3:]
    return pl.pallas_call(
        round_kernel,
        out_shape=pltpu.VMEM((planes, ny, nz), jnp.bfloat16),
        in_specs=[pl.BlockSpec(memory_space=pltpu.HBM)],
        out_specs=pl.BlockSpec(memory_space=pltpu.VMEM),
        scratch_shapes=[pltpu.VMEM((planes, ny, nz), jnp.float32), pltpu.SemaphoreType.DMA((planes,))],
        compiler_params=pltpu.CompilerParams(vmem_limit_bytes=2 * 1024 * 1024),
        cost_estimate=cost(1),
        name="rounded",
    )(in_hbm(fields))


def prepare_kernel(fields, snaps, speed, *refs, planes, ny, nz, splits):
    parts = fields.shape[1]
    refs = list(refs)
    outs = {}
    for c, split in enumerate(splits):
        for piece in range(split):
            if c + piece > 0:
                ref = refs.pop(0)
                for place in range(planes // split):
                    outs[c, piece * planes // split + place] = ref.at[place]
    chunks = [refs.pop(0) for _ in range(parts)]
    coefficients, around_z, buffer, padded, sems, chunk_sems = refs
    copies = {
        (c, i): pltpu.make_async_copy(fields.at[0, c, i], buffer.at[c, i], sems.at[c * planes + i]) for c, i in outs
    }
    count = snaps.shape[0]
    slices = [
        pltpu.make_async_copy(snaps.at[s, c], chunks[c].at[s], chunk_sems.at[c * count + s])
        for c in range(parts)
        for s in range(count)
    ]
    for copy in [*copies.values(), *slices]:
        copy.start()
    base = jnp.broadcast_to(speed[...], (128, ny)).T
    padded[pl.ds(0, PAD), :] = jnp.zeros((PAD, 128), jnp.float32)
    padded[pl.ds(PAD + ny, PAD), :] = jnp.zeros((PAD, 128), jnp.float32)
    padded[pl.ds(PAD, ny), :] = base
    shear = (0.5 * time_step) * (padded[pl.ds(PAD + 1, ny), :] - padded[pl.ds(PAD - 1, ny), :])
    weight = time_step * viscosity
    half = (0.5 * time_step) * base
    for k, scale in enumerate((1.0 / weight, weight)):
        coefficients[3 * k] = scale * (half + weight)
        coefficients[3 * k + 1] = scale * (weight - half)
        coefficients[3 * k + 2] = scale * shear
    apart = lax.broadcasted_iota(jnp.int32, (nz, nz), 0) - lax.broadcasted_iota(jnp.int32, (nz, nz), 1)
    apart = jnp.abs(apart)
    around_z[...] = jnp.where((apart == 1) | (apart == nz - 1), 1.0, 0.0).astype(jnp.bfloat16)
    for c, i in outs:
        copies[c, i].wait()
        outs[c, i][...] = buffer[c, i].astype(jnp.bfloat16)
    for copy in slices:
        copy.wait()


def prepare(fields, snaps, speed, splits):
    _, parts, planes, ny, nz = fields.shape
    count = snaps.shape[0]
    vmem, hbm = pl.BlockSpec(memory_space=pltpu.VMEM), pl.BlockSpec(memory_space=pltpu.HBM)
    outs = [pltpu.VMEM((planes // k, ny, nz), jnp.bfloat16) for split in splits for k in [split] * split][1:]
    pieces = len(outs)
    outs += [pltpu.VMEM((count, planes, ny, nz), snaps.dtype)] * parts
    outs += [pltpu.VMEM((6, ny, 128), jnp.float32), pltpu.VMEM((nz, nz), jnp.bfloat16)]
    got = pl.pallas_call(
        functools.partial(prepare_kernel, planes=planes, ny=ny, nz=nz, splits=splits),
        out_shape=outs,
        in_specs=[hbm, hbm, vmem],
        out_specs=[vmem] * len(outs),
        scratch_shapes=[
            pltpu.VMEM((parts, planes, ny, nz), jnp.float32),
            pltpu.VMEM((ny + 2 * PAD, 128), jnp.float32),
            pltpu.SemaphoreType.DMA((parts * planes,)),
            pltpu.SemaphoreType.DMA((parts * count,)),
        ],
        compiler_params=pltpu.CompilerParams(vmem_limit_bytes=4 * 1024 * 1024),
        cost_estimate=cost(2),
        name="prepare",
    )(in_hbm(fields), in_hbm(snaps), speed[None])
    return list(got[:pieces]), got[pieces : pieces + parts], got[-2], got[-1]


def inner_kernel(*refs, pieces, at):
    run = lax.axis_index("run")
    *refs, out = refs
    snaps, fields = [refs[0:1], refs[1 : 1 + pieces]], refs[1 + pieces :]
    count = fields[0].shape[0]
    planes, ny, _ = refs[0].shape
    pairs = [(k, s) for k in range(len(fields)) for s in range(count)]
    sums = tuple(jnp.zeros((8, 128), jnp.float32) for _ in range(2 * len(pairs)))
    for i in range(planes):

        def body(t, sums, i=i):
            sums = list(sums)
            rows = pl.ds(pl.multiple_of(t * TILE, TILE), TILE)
            for h in (0, 1):
                cols = pl.ds(h * 128, 128)
                mine = []
                for split in snaps:
                    piece, place = i * len(split) // planes, i % (planes // len(split))
                    mine.append(split[piece][place, rows, cols].astype(jnp.float32))
                for p, (k, s) in enumerate(pairs):
                    theirs = fields[k][(s, *at[k], i, rows, cols)].astype(jnp.float32)
                    for j in (0, 1):
                        both = mine[j] * theirs
                        sums[j * len(pairs) + p] = sums[j * len(pairs) + p] + (both[:8] + both[8:])
            return tuple(sums)

        sums = lax.fori_loop(0, ny // TILE, body, sums, unroll=4)
    for j in (0, 1):
        for p, (k, s) in enumerate(pairs):
            out[j, (run ^ k) * count + s] = sums[j * len(pairs) + p]


def inner(first, second, fields, at):
    vmem = pl.BlockSpec(memory_space=pltpu.VMEM)
    operands = [in_vmem(a) for a in (first, *second, *fields)]
    return pl.pallas_call(
        functools.partial(inner_kernel, pieces=len(second), at=at),
        out_shape=jax.ShapeDtypeStruct((2, fields[0].shape[0] * len(fields), 8, 128), jnp.float32),
        in_specs=[vmem] * len(operands),
        out_specs=vmem,
        compiler_params=pltpu.CompilerParams(vmem_limit_bytes=2 * 1024 * 1024),
        cost_estimate=cost(2),
        name="inner",
    )(*operands)


def permute(array, axis, target):
    size = lax.axis_size(axis)
    return lax.ppermute(array, axis, [(i, target(i, size)) for i in range(size)])


def each(arrays, target):
    got = []
    for array in arrays:
        got.append(permute(array, "space", target))
    return tuple(got)


def swap(arrays):
    return each(arrays, lambda i, n: i ^ 1)


def shift(arrays):
    return each(arrays, lambda i, n: (i + 2 - 4 * (i % 2)) % n)


def gather(chunk, c, near, runs):
    got, at = [chunk, *near[1:]], [()] + [(c,)] * (len(near) - 1)
    half = runs // 2
    got.append(permute(chunk, "run", lambda i, n: i ^ half))
    bit = half // 2
    base = {half: got[-1]}
    while bit > 0:
        for k in list(base):
            base[k ^ bit] = permute(base[k], "run", lambda i, n: i ^ bit)
        bit //= 2
    return got[:half] + [base[k] for k in range(half, runs)], at + [()] * (runs - half)


def gather_near(snaps, runs):
    got = {0: snaps}
    bit = runs // 4
    while bit > 0:
        for k in list(got):
            got[k ^ bit] = permute(got[k], "run", lambda i, n: i ^ bit)
        bit //= 2
    return [got[k] for k in range(runs // 2)]


def on_device(adjoint_init, forward_snaps, base_speed, fwd_times, adj_times, horizon):
    runs, spaces = lax.axis_size("run"), lax.axis_size("space")
    _, parts, planes, ny, nz = adjoint_init.shape
    current = [(adjoint_init, (0, c)) for c in range(parts)]
    splits = [SPLITS.get((0, c), 1) for c in range(parts)]
    piece = rounded(adjoint_init, planes // splits[0])
    rest, chunks, coefficients, around_z = prepare(adjoint_init, forward_snaps, base_speed, splits)
    rest = [piece, *rest]
    sent = [tuple(rest.pop(0) for _ in range(split)) for split in splits]
    fields, sums = [], [None] * (SNAP // 2)
    swapped, shifted = {}, {}
    for c in range(parts):
        swapped[0, c] = swap(sent[c])
    near = gather_near(forward_snaps, runs)
    for c in range(parts):
        fields.append(gather(chunks[c], c, near, runs))
    for phase in range(SNAP // 2):
        kept = None
        for c in range(parts):
            if phase > 0:
                swapped[phase, c] = swap(sent[c])
            shifted[phase, c] = shift(swapped[phase, c])
            others = kept if c == 1 else None
            split = SPLITS.get((phase + 1, c), 1)
            halos = swapped[phase, c], shifted[phase, c]
            result = evolve(coefficients, around_z, *current[c], *halos, others, keep=(c == 0), split=split)
            current[c], first = (result[0], ()), result[1]
            sent[c] = tuple(result[2 : 2 + split])
            if c == 0:
                kept = result[2 + split :]
            part = inner(first, sent[c], *fields[c])
            sums[phase] = part if c == 0 else sums[phase] + part
    columns = jnp.stack(sums).reshape(SNAP, -1, 8, 128).sum((2, 3))
    bit = 1
    while bit < spaces:
        columns = columns + permute(columns, "space", lambda i, n: i ^ bit)
        bit *= 2
    summed = columns[None]
    scale = 1.0 / math.sqrt(parts * planes * spaces * ny * nz)
    inside = adj_times[:, :, None] + fwd_times[None, None, :] <= horizon[:, None, None]
    hankel = jnp.where(inside, summed * scale, jnp.zeros_like(summed))
    return (jnp.stack([q for q, _ in current])[None], hankel)


def solution(mesh):
    in_specs = (
        P("run", None, "space", None, None),
        P("run", None, "space", None, None),
        P(),
        P(),
        P("run", None),
        P("run"),
    )
    out_specs = (P("run", None, "space", None, None), P("run", None, None))
    return jax.shard_map(
        on_device, mesh=mesh, in_specs=in_specs, out_specs=out_specs, check_vma=False
    )
```
